128 devices in a mesh: dp: 8 (over z, core), table: 16 (over x, y).
Axes of the slice: x: 4, y: 4, z: 4, core: 2. Of those that a mesh axis runs over, the one named last changes fastest.
Arguments:
- values: bfloat16 [16384, 1024], P('table'), may hold values from -6 to 6
- first_moment: float32 [16384, 1024], P('table'), may hold values from -2 to 2
- second_moment: float32 [16384, 1024], P('table'), may hold values from 0.01 to 1
- grads: bfloat16 [1024, 64, 1024], P(('dp', 'table')), may hold values from -6 to 6
- block_ids: int32 [128, 8], P(('dp', 'table')), may hold values from 0 to 255, as said below
- live_counts: int32 [128], P(('dp', 'table')), may hold values from 4 to 8
- step_count: int32 [1], replicated, may hold values from 1 to 19
Outputs:
- new_values: bfloat16 [16384, 1024], P('table')
- new_first: float32 [16384, 1024], P('table')
- new_second: float32 [16384, 1024], P('table')
The draws below stay inside these ranges and needn't reach their ends.
Inputs may be any that keep to these rules, and one draw needn't show every extreme that they name: `block_ids`: device h belongs to replica h // 16. Live ids of a device are ascending and lie in blocks of different owners (owner = id // 16), so one device sends at most one live block to any owner; in every draw some owner receives a live block from every device of a replica. The live ids of one replica name at most 2 different blocks of any one owner, and exactly 2 of some owner in every replica. Ids of dead slots are arbitrary blocks.
All inputs are finite; a program needn't handle non-finite values.
Results may differ from the reference program's by a relative error of at most 0.0004.
Values may be sent and summed in bfloat16 or wider, within the bound.
A program may use at most 128 MiB of HBM per device.

```python
import math
import jax
import jax.numpy as jnp

D = 1024
BROWS = 64
SLOTS = 8
BLK_DEV = 16
NBLK = 256
ROWS = 16384
HOLDERS = 128
GSLOTS = 1024


def draw_pair(key):
    key = jax.random.fold_in(key, 7)
    keys = jax.random.split(key, 7)
    owners = NBLK // BLK_DEV
    replicas = HOLDERS // owners
    holder = jnp.arange(HOLDERS, dtype=jnp.int32)
    replica = holder // owners
    column = holder % owners
    hot = jax.random.randint(keys[0], (replicas,), 0, owners)[replica]
    scores = jax.random.randint(keys[1], (HOLDERS, owners - 1), 0, 1 << 20) * owners + jnp.arange(owners - 1, dtype=jnp.int32)[None, :]
    offsets = jnp.argsort(scores, axis=1)[:, :SLOTS - 1].astype(jnp.int32) + 1
    chosen = jnp.concatenate([hot[:, None], (hot[:, None] + offsets) % owners], axis=1)
    pair_first = jax.random.randint(keys[2], (replicas, owners), 0, BLK_DEV)
    pair_second = (pair_first + 1 + jax.random.randint(keys[3], (replicas, owners), 0, BLK_DEV - 1)) % BLK_DEV
    picks = jax.random.randint(keys[4], (HOLDERS, SLOTS - 1), 0, 2)
    picks = jnp.concatenate([(column % 2)[:, None], picks], axis=1)
    option_one = pair_first[replica[:, None], chosen]
    option_two = pair_second[replica[:, None], chosen]
    local = jnp.where(picks == 0, option_one, option_two)
    named = chosen * BLK_DEV + local
    counts = jax.random.randint(keys[5], (HOLDERS,), SLOTS // 2, SLOTS + 1)
    filler = jax.random.randint(keys[6], (HOLDERS, SLOTS), 0, NBLK)
    live = jnp.arange(SLOTS, dtype=jnp.int32)[None, :] < counts[:, None]
    keyed = jnp.where(live, named, NBLK + filler)
    ordered = jnp.sort(keyed, axis=1)
    result = jnp.where(ordered < NBLK, ordered, ordered - NBLK)
    return (result.astype(jnp.int32), counts.astype(jnp.int32))


def draw_block_ids(key, part):
    return draw_pair(key)[0]


def draw_live_counts(key, part):
    return draw_pair(key)[1]


def levels(own_key, dims, shards, smallest, largest):
    level = 1.0
    for position, shards_of in shards:
        draws = jax.random.uniform(jax.random.fold_in(jax.random.fold_in(own_key, 6), position), (shards_of,), jnp.float32, smallest / len(shards), largest / len(shards))
        level = level * jnp.repeat(jnp.exp(draws), dims[position] // shards_of).reshape((-1,) + (1,) * (len(dims) - 1 - position))
    return level


def gaussian(key, extent, width, limit, shards=(), held_as=jnp.bfloat16):
    factor_of = levels(key, extent, shards, -0.22, 0.18) if shards else 1.0
    values = jax.random.normal(key, extent, jnp.float32) * width * factor_of
    return jnp.minimum(jnp.maximum(values, -limit), limit).astype(held_as)


def setup_inputs(seed: int = 0) -> dict:
    seeds = jax.random.split(jax.random.key(seed), 8)
    return {
        "values": gaussian(seeds[0], (ROWS, D), 1.0, 6.0, ((0, 16),)),
        "first_moment": gaussian(seeds[1], (ROWS, D), 0.3, 2.0, ((0, 16),), jnp.float32),
        "second_moment": jnp.clip(jnp.exp(math.log(1.0) - 4.6051702 * jax.random.uniform(seeds[2], (ROWS, D), jnp.float32) ** levels(seeds[2], (ROWS, D), ((0, 16),), -0.2, 0.2)), 0.01, 1.0),
        "grads": gaussian(seeds[3], (GSLOTS, BROWS, D), 1.0, 6.0, ((0, 128),)),
        "block_ids": draw_block_ids(jax.random.fold_in(seeds[7], 71), 0),
        "live_counts": draw_live_counts(jax.random.fold_in(seeds[7], 71), 0),
        "step_count": jax.random.randint(seeds[6], (1,), 1, 20).astype(jnp.int32),
    }


def reference(values, first_moment, second_moment, grads, block_ids, live_counts, step_count):
    live = (jnp.arange(SLOTS, dtype=jnp.int32)[None, :] < live_counts[:, None]).reshape(-1)
    flat_ids = block_ids.reshape(-1).astype(jnp.int32)
    weight = live.astype(jnp.float32)
    summed = jax.ops.segment_sum(grads.astype(jnp.float32) * weight[:, None, None], flat_ids, NBLK)
    row_grad = summed.reshape(ROWS, D)
    hits = jax.ops.segment_sum(weight, flat_ids, NBLK)
    touched = (jnp.repeat(hits, BROWS) > 0.0)[:, None]
    beta_one = 0.9
    beta_two = 0.99
    steps_done = step_count[0].astype(jnp.float32)
    first_next = beta_one * first_moment + (1.0 - beta_one) * row_grad
    second_next = beta_two * second_moment + (1.0 - beta_two) * row_grad * row_grad
    first_hat = first_next / (1.0 - jnp.power(jnp.float32(beta_one), steps_done))
    second_hat = second_next / (1.0 - jnp.power(jnp.float32(beta_two), steps_done))
    moved = values.astype(jnp.float32) - 0.05 * first_hat / (jnp.sqrt(second_hat) + 1e-08)
    new_values = jnp.where(touched, moved.astype(jnp.bfloat16), values)
    new_first = jnp.where(touched, first_next, first_moment)
    new_second = jnp.where(touched, second_next, second_moment)
    return (new_values, new_first, new_second)
```

```python
import functools

import jax
import jax.numpy as jnp
from jax import lax
from jax.experimental import pallas as pl
from jax.experimental.pallas import tpu as pltpu
from jax.sharding import PartitionSpec as P

MESH = pl.DeviceIdType.MESH
BROWS = 64
SLOTS = 8
NSIDE = 4
NC = 4
RB = BROWS // NC
PLANE = [(dx, dy) for dx in range(4) for dy in range(4) if (dx, dy) != (0, 0)]
NP = len(PLANE)
NREP = 8
NOBLK = 1 << 20


def exchange_kernel(
    ids_ref, cnt_ref, grads_hbm,
    gath, idg,
    grads, stage, inc, lab_out, lab_in,
    ld_sem, lab_ss, lab_rs, a_ss, a_rs, id_ss, id_rs, b_ss, b_rs, f_ss, f_rs, s_ss, s_rs,
):
    dp = lax.axis_index("dp")
    tb = lax.axis_index("table")
    z, core = dp // 2, dp % 2
    x, y = tb // NSIDE, tb % NSIDE
    width = grads.shape[2]

    def plane_peer(i):
        dx, dy = PLANE[i]
        return ((x + dx) % NSIDE) * NSIDE + (y + dy) % NSIDE

    def rep_peer(dz, dc):
        return ((z + dz) % NSIDE) * 2 + (core + dc) % 2

    owners = [plane_peer(i) for i in range(NP)] + [tb]
    dp_peers = [(dz, dc) for dz in range(NSIDE) for dc in range(2) if (dz, dc) != (0, 0)]

    load = pltpu.make_async_copy(grads_hbm, grads, ld_sem)
    load.start()

    barrier = pltpu.get_barrier_semaphore()
    for i in range(NP):
        pl.semaphore_signal(barrier, inc=1, device_id=(dp, owners[i]), device_id_type=MESH)
    for dz, dc in dp_peers:
        pl.semaphore_signal(barrier, inc=1, device_id=(rep_peer(dz, dc), tb), device_id_type=MESH)

    count = cnt_ref[0]
    named = [jnp.where(s < count, ids_ref[0, s], NOBLK) for s in range(SLOTS)]
    slot_of = []
    for i in range(NP + 1):
        slot = jnp.int32(0)
        label = jnp.int32(-1)
        for s in range(SLOTS):
            here = (named[s] >> 4) == owners[i]
            slot = jnp.where(here, s, slot)
            label = jnp.where(here, named[s] & 15, label)
        slot_of.append(slot)
        row = jnp.full((1, width), label, jnp.int32)
        if i < NP:
            lab_out[i] = row
        else:
            lab_in[i] = row

    pl.semaphore_wait(barrier, NP + len(dp_peers))

    def label_copy(i):
        return pltpu.make_async_remote_copy(
            src_ref=lab_out.at[i], dst_ref=lab_in.at[i], send_sem=lab_ss.at[i], recv_sem=lab_rs.at[i],
            device_id=(dp, owners[i]), device_id_type=MESH)

    def block_copy(c, i):
        return pltpu.make_async_remote_copy(
            src_ref=stage.at[c, i], dst_ref=inc.at[c, i], send_sem=a_ss.at[c, i], recv_sem=a_rs.at[c, i],
            device_id=(dp, owners[i]), device_id_type=MESH)

    for i in range(NP):
        label_copy(i).start()
    load.wait()

    @pl.loop(0, NC)
    def _(c):
        rows = pl.ds(pl.multiple_of(c * RB, RB), RB)
        for i in range(NP):
            stage[c, i] = grads[slot_of[i], rows, :]
            block_copy(c, i).start()
        inc[c, NP] = grads[slot_of[NP], rows, :]

    for i in range(NP):
        label_copy(i).wait()
    low = jnp.full((1, width), NOBLK, jnp.int32)
    high = jnp.full((1, width), -1, jnp.int32)
    for i in range(NP + 1):
        lab = lab_in[i]
        low = jnp.minimum(low, jnp.where(lab < 0, NOBLK, lab))
        high = jnp.maximum(high, lab)
    two = high > low
    idg[dp, 0:1] = jnp.where(low < NOBLK, low, -1)[:, :128]
    idg[dp, 1:2] = jnp.where(two, high, -1)[:, :128]

    def id_copy(j):
        dz, dc = dp_peers[j]
        return pltpu.make_async_remote_copy(
            src_ref=idg.at[dp], dst_ref=idg.at[dp], send_sem=id_ss.at[j], recv_sem=id_rs.at[j],
            device_id=(rep_peer(dz, dc), tb), device_id_type=MESH)

    for j in range(len(dp_peers)):
        id_copy(j).start()

    def ring_copy(c, j):
        return pltpu.make_async_remote_copy(
            src_ref=gath.at[c, dp], dst_ref=gath.at[c, dp], send_sem=b_ss.at[c, j], recv_sem=b_rs.at[c, j],
            device_id=(rep_peer(1 if j == 0 else 3, 0), tb), device_id_type=MESH)

    def forward_copy(c, j):
        origin = rep_peer(3 if j == 0 else 1, 0)
        return pltpu.make_async_remote_copy(
            src_ref=gath.at[c, origin, j], dst_ref=gath.at[c, origin, j], send_sem=f_ss.at[c, j], recv_sem=f_rs.at[c, j],
            device_id=(rep_peer(1 if j == 0 else 3, 0), tb), device_id_type=MESH)

    def core_copy(c, dz):
        origin = rep_peer(dz, 0)
        return pltpu.make_async_remote_copy(
            src_ref=gath.at[c, origin], dst_ref=gath.at[c, origin], send_sem=s_ss.at[c, dz], recv_sem=s_rs.at[c, dz],
            device_id=(rep_peer(0, 1), tb), device_id_type=MESH)

    def second_hop(c):
        for j in range(2):
            ring_copy(c, j).wait_recv()
            forward_copy(c, j).start()
            core_copy(c, 3 if j == 0 else 1).start()

    def third_hop(c):
        for j in range(2):
            forward_copy(c, j).wait_recv()
        core_copy(c, 2).start()

    @pl.loop(0, NC)
    def _(c):
        for i in range(NP):
            block_copy(c, i).wait_recv()
        sum_low = jnp.zeros((RB, width), jnp.float32)
        sum_high = jnp.zeros((RB, width), jnp.float32)
        for i in range(NP + 1):
            lab = lab_in[i]
            block = inc[c, i].astype(jnp.float32)
            sum_low += jnp.where(lab == low, 1.0, 0.0) * block
            sum_high += jnp.where((lab == high) & two, 1.0, 0.0) * block
        gath[c, dp, 0] = sum_low
        gath[c, dp, 1] = sum_high
        for j in range(2):
            ring_copy(c, j).start()
        core_copy(c, 0).start()

        @pl.when(c >= 1)
        def _():
            second_hop(c - 1)

        @pl.when(c >= 2)
        def _():
            third_hop(c - 2)

    third_hop(NC - 2)
    second_hop(NC - 1)
    third_hop(NC - 1)

    for j in range(len(dp_peers)):
        id_copy(j).wait()

    @pl.loop(0, NC)
    def _(c):
        for dz in range(NSIDE):
            core_copy(c, dz).wait()
        for j in range(2):
            ring_copy(c, j).wait_send()
            forward_copy(c, j).wait_send()
        for i in range(NP):
            block_copy(c, i).wait_send()


def adam_kernel(
    ids_ref, scale_ref, gath, values, first, second,
    out_v, out_f, out_s,
    grad, new_v, new_f, new_s, hit, sem,
):
    nblk = grad.shape[0]
    for b in range(nblk):
        hit[b] = 0
    for r in range(NREP):
        for k in range(2):
            b = ids_ref[r, k, 0]

            @pl.when(b >= 0)
            def _():
                @pl.when(hit[b] == 0)
                def _():
                    for c in range(NC):
                        grad[b, c] = gath[c, r, k]

                @pl.when(hit[b] > 0)
                def _():
                    for c in range(NC):
                        grad[b, c] += gath[c, r, k]

                hit[b] = 1

    inv_one = scale_ref[0]
    inv_two = scale_ref[1]

    def copies(b, v, f, s):
        rows = pl.ds(pl.multiple_of(b * BROWS, BROWS), BROWS)
        return [
            pltpu.make_async_copy(v.at[rows], out_v.at[rows], sem.at[0, b]),
            pltpu.make_async_copy(f.at[rows], out_f.at[rows], sem.at[1, b]),
            pltpu.make_async_copy(s.at[rows], out_s.at[rows], sem.at[2, b]),
        ]

    @pl.loop(0, nblk)
    def _(b):
        @pl.when(hit[b] > 0)
        def _():
            for c in range(NC):
                rows = pl.ds(pl.multiple_of(b * BROWS + c * RB, RB), RB)
                g = grad[b, c]
                f = 0.9 * first[rows, :] + (1.0 - 0.9) * g
                s = 0.99 * second[rows, :] + (1.0 - 0.99) * g * g
                new_f[rows, :] = f
                new_s[rows, :] = s
                moved = values[rows, :].astype(jnp.float32) - 0.05 * (f / inv_one) / (jnp.sqrt(s / inv_two) + 1e-08)
                new_v[rows, :] = moved.astype(jnp.bfloat16)
            for cp in copies(b, new_v, new_f, new_s):
                cp.start()

        @pl.when(hit[b] == 0)
        def _():
            for cp in copies(b, values, first, second):
                cp.start()

    @pl.loop(0, nblk)
    def _(b):
        for cp in copies(b, new_v, new_f, new_s):
            cp.wait()


def per_device(values, first_moment, second_moment, grads, block_ids, live_counts, step_count):
    own_rows, width = values.shape
    nblk = own_rows // BROWS
    dma = pltpu.SemaphoreType.DMA
    vmem = pl.BlockSpec(memory_space=pltpu.VMEM)
    smem = pl.BlockSpec(memory_space=pltpu.SMEM)
    hbm = pl.BlockSpec(memory_space=pl.ANY)
    gath, ids = pl.pallas_call(
        exchange_kernel,
        out_shape=(
            jax.ShapeDtypeStruct((NC, NREP, 2, RB, width), jnp.float32),
            jax.ShapeDtypeStruct((NREP, 2, 128), jnp.int32),
        ),
        in_specs=[smem, smem, hbm],
        out_specs=(vmem, vmem),
        scratch_shapes=[
            pltpu.VMEM((SLOTS, BROWS, width), jnp.bfloat16),
            pltpu.VMEM((NC, NP, RB, width), jnp.bfloat16),
            pltpu.VMEM((NC, NP + 1, RB, width), jnp.bfloat16),
            pltpu.VMEM((NP, 1, width), jnp.int32),
            pltpu.VMEM((NP + 1, 1, width), jnp.int32),
            dma(()), dma((NP,)), dma((NP,)), dma((NC, NP)), dma((NC, NP)),
            dma((NREP - 1,)), dma((NREP - 1,)), dma((NC, 2)), dma((NC, 2)),
            dma((NC, 2)), dma((NC, 2)), dma((NC, NSIDE)), dma((NC, NSIDE)),
        ],
        compiler_params=pltpu.CompilerParams(
            collective_id=0, has_side_effects=True, vmem_limit_bytes=24 << 20),
        name="exchange",
    )(block_ids, live_counts, grads)
    steps = step_count[0].astype(jnp.float32)
    scales = jnp.stack([1.0 - jnp.power(jnp.float32(0.9), steps), 1.0 - jnp.power(jnp.float32(0.99), steps)])
    return pl.pallas_call(
        adam_kernel,
        out_shape=tuple(jax.ShapeDtypeStruct(a.shape, a.dtype) for a in (values, first_moment, second_moment)),
        in_specs=[smem, smem, vmem, vmem, vmem, vmem],
        out_specs=(hbm, hbm, hbm),
        scratch_shapes=[
            pltpu.VMEM((nblk, NC, RB, width), jnp.float32),
            pltpu.VMEM((own_rows, width), jnp.bfloat16),
            pltpu.VMEM((own_rows, width), jnp.float32),
            pltpu.VMEM((own_rows, width), jnp.float32),
            pltpu.SMEM((nblk,), jnp.int32),
            dma((3, nblk)),
        ],
        compiler_params=pltpu.CompilerParams(vmem_limit_bytes=40 << 20),
        name="adam",
    )(ids, scales, gath, values, first_moment, second_moment)


def solution(mesh):
    in_specs = (
        P("table", None),
        P("table", None),
        P("table", None),
        P(("dp", "table"), None, None),
        P(("dp", "table"), None),
        P(("dp", "table")),
        P(),
    )
    out_specs = (P("table", None), P("table", None), P("table", None))
    return jax.shard_map(
        per_device, mesh=mesh, in_specs=in_specs, out_specs=out_specs, check_vma=False
    )
```

```python
import jax
import jax.numpy as jnp
from jax import lax
from jax.experimental import pallas as pl
from jax.experimental.pallas import tpu as pltpu
from jax.sharding import PartitionSpec as P

MESH = pl.DeviceIdType.MESH
BROWS = 64
SLOTS = 8
NSIDE = 4
NC = 4
RB = BROWS // NC
PLANE = [(1, 2), (0, 1), (1, 1), (0, 2), (3, 2), (0, 3), (3, 3), (2, 0), (2, 1), (1, 0), (1, 3), (2, 2), (2, 3), (3, 0), (3, 1)]
NP = len(PLANE)
NREP = 8
NOBLK = 1 << 20


def exchange_kernel(
    cnt_ref, step_ref, ids_hbm, grads_hbm, values_hbm, first_hbm, second_hbm,
    gath, idg, values, first, second,
    ids_ref, grads, stage, inc, lab_out, lab_in,
    sm_sem, ld_sem, lab_ss, lab_rs, a_ss, a_rs, id_ss, id_rs, b_ss, b_rs, s_ss, s_rs,
):
    dp = lax.axis_index("dp")
    tb = lax.axis_index("table")
    z, core = dp // 2, dp % 2
    x, y = tb // NSIDE, tb % NSIDE
    width = grads.shape[2]

    def plane_peer(i):
        dx, dy = PLANE[i]
        return ((x + dx) % NSIDE) * NSIDE + (y + dy) % NSIDE

    def rep_peer(dz, dc):
        return ((z + dz) % NSIDE) * 2 + (core + dc) % 2

    owners = [plane_peer(i) for i in range(NP)] + [tb]
    dp_peers = [(dz, dc) for dz in range(NSIDE) for dc in range(2) if (dz, dc) != (0, 0)]

    small = [
        pltpu.make_async_copy(ids_hbm, ids_ref, sm_sem.at[0]),
    ]
    load = pltpu.make_async_copy(grads_hbm, grads, ld_sem.at[0])
    held = [
        pltpu.make_async_copy(values_hbm, values, ld_sem.at[1]),
        pltpu.make_async_copy(first_hbm, first, ld_sem.at[2]),
        pltpu.make_async_copy(second_hbm, second, ld_sem.at[3]),
    ]
    for cp in small:
        cp.start()
    load.start()

    barrier = pltpu.get_barrier_semaphore()
    for i in range(NP):
        pl.semaphore_signal(barrier, inc=1, device_id=(dp, owners[i]), device_id_type=MESH)
    for dz, dc in dp_peers:
        pl.semaphore_signal(barrier, inc=1, device_id=(rep_peer(dz, dc), tb), device_id_type=MESH)

    for cp in small:
        cp.wait()
    count = cnt_ref[0]
    named = [jnp.where(s < count, ids_ref[0, s], NOBLK) for s in range(SLOTS)]
    slot_of = []
    for i in range(NP + 1):
        slot = jnp.int32(0)
        label = jnp.int32(-1)
        for s in range(SLOTS):
            here = (named[s] >> 4) == owners[i]
            slot = jnp.where(here, s, slot)
            label = jnp.where(here, named[s] & 15, label)
        slot_of.append(slot)
        row = jnp.full((1, width), label, jnp.int32)
        if i < NP:
            lab_out[i] = row
        else:
            lab_in[i] = row

    load.wait()
    pl.semaphore_wait(barrier, NP + len(dp_peers))

    def label_copy(i):
        return pltpu.make_async_remote_copy(
            src_ref=lab_out.at[i], dst_ref=lab_in.at[i], send_sem=lab_ss.at[i], recv_sem=lab_rs.at[i],
            device_id=(dp, owners[i]), device_id_type=MESH)

    def block_copy(c, i):
        return pltpu.make_async_remote_copy(
            src_ref=stage.at[c, i], dst_ref=inc.at[c, i], send_sem=a_ss.at[c], recv_sem=a_rs.at[c],
            device_id=(dp, owners[i]), device_id_type=MESH)

    def all_blocks(c):
        blocks = pl.ds(0, NP)
        return pltpu.make_async_remote_copy(
            src_ref=stage.at[c, blocks], dst_ref=inc.at[c, blocks], send_sem=a_ss.at[c], recv_sem=a_rs.at[c],
            device_id=(dp, owners[0]), device_id_type=MESH)

    def send_blocks(c):
        rows = pl.ds(pl.multiple_of(c * RB, RB), RB)
        for i in range(NP):
            stage[c, i] = grads[slot_of[i], rows, :]
            block_copy(c, i).start()
        inc[c, NP] = grads[slot_of[NP], rows, :]

    send_blocks(0)
    for i in range(NP):
        label_copy(i).start()

    @pl.loop(1, NC)
    def _(c):
        send_blocks(c)

    for cp in held:
        cp.start()

    for i in range(NP):
        label_copy(i).wait()
    low = jnp.full((1, width), NOBLK, jnp.int32)
    high = jnp.full((1, width), -1, jnp.int32)
    for i in range(NP + 1):
        lab = lab_in[i]
        low = jnp.minimum(low, jnp.where(lab < 0, NOBLK, lab))
        high = jnp.maximum(high, lab)
    two = high > low
    idg[dp, 0:1] = jnp.where(low < NOBLK, low, -1)[:, :128]
    idg[dp, 1:2] = jnp.where(two, high, -1)[:, :128]
    idg[NREP] = jnp.full((2, 128), step_ref[0], jnp.int32)

    def id_copy(j):
        dz, dc = dp_peers[j]
        return pltpu.make_async_remote_copy(
            src_ref=idg.at[dp], dst_ref=idg.at[dp], send_sem=id_ss.at[j], recv_sem=id_rs.at[j],
            device_id=(rep_peer(dz, dc), tb), device_id_type=MESH)

    for j in range(len(dp_peers)):
        id_copy(j).start()

    def ring_copy(c, dz):
        return pltpu.make_async_remote_copy(
            src_ref=gath.at[c, dp], dst_ref=gath.at[c, dp], send_sem=b_ss.at[c, dz - 1], recv_sem=b_rs.at[c, dz - 1],
            device_id=(rep_peer(dz, 0), tb), device_id_type=MESH)

    def core_copy(c, dz):
        origin = rep_peer(dz, 0)
        return pltpu.make_async_remote_copy(
            src_ref=gath.at[c, origin], dst_ref=gath.at[c, origin], send_sem=s_ss.at[c, dz], recv_sem=s_rs.at[c, dz],
            device_id=(rep_peer(0, 1), tb), device_id_type=MESH)

    def second_hop(c):
        for dz in (1, 3, 2):
            ring_copy(c, dz).wait_recv()
            core_copy(c, NSIDE - dz).start()

    @pl.loop(0, NC)
    def _(c):
        all_blocks(c).wait_recv()
        sum_low = jnp.zeros((RB, width), jnp.float32)
        sum_high = jnp.zeros((RB, width), jnp.float32)
        for i in range(NP + 1):
            lab = lab_in[i]
            block = inc[c, i].astype(jnp.float32)
            sum_low += jnp.where(lab == low, 1.0, 0.0) * block
            sum_high += jnp.where((lab == high) & two, 1.0, 0.0) * block
        gath[c, dp, 0] = sum_low
        gath[c, dp, 1] = sum_high
        for dz in (1, 3, 2):
            ring_copy(c, dz).start()
        core_copy(c, 0).start()

        @pl.when(c >= 1)
        def _():
            second_hop(c - 1)

    second_hop(NC - 1)

    for j in range(len(dp_peers)):
        id_copy(j).wait()
    for cp in held:
        cp.wait()

    @pl.loop(0, NC)
    def _(c):
        for dz in range(NSIDE):
            core_copy(c, dz).wait()
        for dz in range(1, NSIDE):
            ring_copy(c, dz).wait_send()
        all_blocks(c).wait_send()


def adam_kernel(
    ids_ref, gath, values, first, second,
    out_v, out_f, out_s,
    tmp, new_v, new_f, new_s, count, names, sem,
):
    nblk = values.shape[0] // BROWS
    for b in range(nblk + 1):
        count[b] = 0
    for q in range(2 * NREP):
        named = ids_ref[q // 2, q % 2, 0]
        b = jnp.where(named < 0, nblk, named)
        n = count[b]
        names[b * 2 * NREP + n] = q
        count[b] = n + 1

    steps = ids_ref[NREP, 0, 0]
    power_one, power_two = lax.fori_loop(
        0, steps, lambda _, p: (p[0] * 0.9, p[1] * 0.99), (jnp.float32(1.0), jnp.float32(1.0)))
    one = jnp.full((1, 1024), 1.0 - power_one, jnp.float32)
    two = jnp.full((1, 1024), 1.0 - power_two, jnp.float32)
    rate = 0.05 / one
    scale = 1.0 / two

    def copies(b, v, f, s):
        rows = pl.ds(pl.multiple_of(b * BROWS, BROWS), BROWS)
        return [
            pltpu.make_async_copy(v.at[rows], out_v.at[rows], sem.at[0, b]),
            pltpu.make_async_copy(f.at[rows], out_f.at[rows], sem.at[1, b]),
            pltpu.make_async_copy(s.at[rows], out_s.at[rows], sem.at[2, b]),
        ]

    def update(b, grad_of):
        for c in range(NC):
            rows = pl.ds(pl.multiple_of(b * BROWS + c * RB, RB), RB)
            g = grad_of(c)
            f = 0.9 * first[rows, :] + (1.0 - 0.9) * g
            s = 0.99 * second[rows, :] + (1.0 - 0.99) * g * g
            new_f[rows, :] = f
            new_s[rows, :] = s
            moved = values[rows, :].astype(jnp.float32) - rate * f / (jnp.sqrt(scale * s) + 1e-08)
            new_v[rows, :] = moved.astype(jnp.bfloat16)
        for cp in copies(b, new_v, new_f, new_s):
            cp.start()

    @pl.loop(0, nblk)
    def _(b):
        @pl.when(count[b] == 0)
        def _():
            for cp in copies(b, values, first, second):
                cp.start()

    @pl.loop(0, nblk)
    def _(b):
        n = count[b]
        base = b * 2 * NREP

        def name_of(j):
            q = names[base + j]
            return q >> 1, q & 1

        @pl.when(n == 1)
        def _():
            r, k = name_of(0)
            update(b, lambda c: gath[c, r, k])

        @pl.when(n > 1)
        def _():
            r, k = name_of(0)
            r1, k1 = name_of(1)
            for c in range(NC):
                tmp[c] = gath[c, r, k] + gath[c, r1, k1]

            def more(j, _):
                rj, kj = name_of(j)
                for c in range(NC):
                    tmp[c] += gath[c, rj, kj]
                return 0

            lax.fori_loop(2, n, more, 0)
            update(b, lambda c: tmp[c])

    @pl.loop(0, nblk)
    def _(b):
        for cp in copies(b, new_v, new_f, new_s):
            cp.wait()


def per_device(values, first_moment, second_moment, grads, block_ids, live_counts, step_count):
    own_rows, width = values.shape
    nblk = own_rows // BROWS
    dma = pltpu.SemaphoreType.DMA
    vmem = pl.BlockSpec(memory_space=pltpu.VMEM)
    smem = pl.BlockSpec(memory_space=pltpu.SMEM)
    hbm = pl.BlockSpec(memory_space=pltpu.HBM)
    like = lambda a: jax.ShapeDtypeStruct(a.shape, a.dtype)
    gath, ids, values_in, first_in, second_in = pl.pallas_call(
        exchange_kernel,
        out_shape=(
            jax.ShapeDtypeStruct((NC, NREP, 2, RB, width), jnp.float32),
            jax.ShapeDtypeStruct((NREP + 1, 2, 128), jnp.int32),
            like(values), like(first_moment), like(second_moment),
        ),
        in_specs=[smem, smem] + [hbm] * 5,
        out_specs=(vmem,) * 5,
        scratch_shapes=[
            pltpu.SMEM(block_ids.shape, jnp.int32),
            pltpu.VMEM((SLOTS, BROWS, width), jnp.bfloat16),
            pltpu.VMEM((NC, NP, RB, width), jnp.bfloat16),
            pltpu.VMEM((NC, NP + 1, RB, width), jnp.bfloat16),
            pltpu.VMEM((NP, 1, width), jnp.int32),
            pltpu.VMEM((NP + 1, 1, width), jnp.int32),
            dma((3,)), dma((4,)), dma((NP,)), dma((NP,)), dma((NC,)), dma((NC,)),
            dma((NREP - 1,)), dma((NREP - 1,)), dma((NC, NSIDE - 1)), dma((NC, NSIDE - 1)),
            dma((NC, NSIDE)), dma((NC, NSIDE)),
        ],
        compiler_params=pltpu.CompilerParams(
            collective_id=0, has_side_effects=True, vmem_limit_bytes=24 << 20),
        name="exchange",
    )(live_counts, step_count, *[pltpu.with_memory_space_constraint(a, pltpu.HBM) for a in (block_ids, grads, values, first_moment, second_moment)])
    return pl.pallas_call(
        adam_kernel,
        out_shape=(like(values), like(first_moment), like(second_moment)),
        in_specs=[smem, vmem, vmem, vmem, vmem],
        out_specs=(hbm, hbm, hbm),
        scratch_shapes=[
            pltpu.VMEM((NC, RB, width), jnp.float32),
            pltpu.VMEM((own_rows, width), jnp.bfloat16),
            pltpu.VMEM((own_rows, width), jnp.float32),
            pltpu.VMEM((own_rows, width), jnp.float32),
            pltpu.SMEM((nblk + 1,), jnp.int32),
            pltpu.SMEM(((nblk + 1) * 2 * NREP,), jnp.int32),
            dma((3, nblk)),
        ],
        compiler_params=pltpu.CompilerParams(vmem_limit_bytes=24 << 20),
        name="adam",
    )(ids, gath, values_in, first_in, second_in)


def solution(mesh):
    in_specs = (
        P("table", None),
        P("table", None),
        P("table", None),
        P(("dp", "table"), None, None),
        P(("dp", "table"), None),
        P(("dp", "table")),
        P(),
    )
    out_specs = (P("table", None), P("table", None), P("table", None))
    return jax.shard_map(
        per_device, mesh=mesh, in_specs=in_specs, out_specs=out_specs, check_vma=False
    )
```

```python
import jax
import jax.numpy as jnp
from jax import lax
from jax.experimental import pallas as pl
from jax.experimental.pallas import tpu as pltpu
from jax.sharding import PartitionSpec as P

MESH = pl.DeviceIdType.MESH
BROWS = 64
SLOTS = 8
NSIDE = 4
RB = 16
CW = 256
NROW = BROWS // RB
NCOL = 1024 // CW
NC = NROW * NCOL
PLANE = [(2, 2), (1, 2), (3, 2), (2, 1), (2, 3), (1, 1), (3, 3), (1, 3), (3, 1), (0, 2), (2, 0), (0, 1), (0, 3), (1, 0), (3, 0)]
NP = len(PLANE)
NREP = 8
LAST = (4, 3, 2, 5, 1, 6, 0)
LAG = 5
NOBLK = 1 << 20


def exchange_kernel(
    cnt_ref, step_ref, ids_hbm, grads_hbm, values_hbm, first_hbm, second_hbm,
    gath, idg, values, first, second,
    ids_ref, grads, stage, inc, lab_out, lab_in, weight,
    sm_sem, ld_sem, lab_ss, lab_rs, a_ss, a_rs, id_ss, id_rs, b_ss, b_rs, s_ss, s_rs, l_ss, l_rs,
):
    dp = lax.axis_index("dp")
    tb = lax.axis_index("table")
    z, core = dp // 2, dp % 2
    x, y = tb // NSIDE, tb % NSIDE

    def plane_peer(i):
        dx, dy = PLANE[i]
        return ((x + dx) % NSIDE) * NSIDE + (y + dy) % NSIDE

    def rep_peer(dz, dc):
        return ((z + dz) % NSIDE) * 2 + (core + dc) % 2

    owners = [plane_peer(i) for i in range(NP)] + [tb]
    dp_peers = [(dz, dc) for dz in range(NSIDE) for dc in range(2) if (dz, dc) != (0, 0)]

    small = [
        pltpu.make_async_copy(ids_hbm, ids_ref, sm_sem.at[0]),
    ]
    load = pltpu.make_async_copy(grads_hbm, grads, ld_sem.at[0])
    held = [
        pltpu.make_async_copy(values_hbm, values, ld_sem.at[1]),
        pltpu.make_async_copy(first_hbm, first, ld_sem.at[2]),
        pltpu.make_async_copy(second_hbm, second, ld_sem.at[3]),
    ]
    for cp in small:
        cp.start()
    load.start()

    barrier = pltpu.get_barrier_semaphore()
    for i in range(NP):
        pl.semaphore_signal(barrier, inc=1, device_id=(dp, owners[i]), device_id_type=MESH)
    for dz, dc in dp_peers:
        pl.semaphore_signal(barrier, inc=1, device_id=(rep_peer(dz, dc), tb), device_id_type=MESH)

    for cp in small:
        cp.wait()
    count = cnt_ref[0]
    named = [jnp.where(s < count, ids_ref[0, s], NOBLK) for s in range(SLOTS)]
    slot_of = []
    for i in range(NP + 1):
        slot = jnp.int32(0)
        label = jnp.int32(-1)
        for s in range(SLOTS):
            here = (named[s] >> 4) == owners[i]
            slot = jnp.where(here, s, slot)
            label = jnp.where(here, named[s] & 15, label)
        slot_of.append(slot)
        row = jnp.full((1, CW), label, jnp.int32)
        if i < NP:
            lab_out[i] = row
        else:
            lab_in[i] = row

    load.wait()
    pl.semaphore_wait(barrier, NP + len(dp_peers))

    def label_copy(i):
        return pltpu.make_async_remote_copy(
            src_ref=lab_out.at[i], dst_ref=lab_in.at[i], send_sem=lab_ss, recv_sem=lab_rs,
            device_id=(dp, owners[i]), device_id_type=MESH)

    def block_copy(c, i):
        return pltpu.make_async_remote_copy(
            src_ref=stage.at[c, i], dst_ref=inc.at[c, i], send_sem=a_ss, recv_sem=a_rs.at[c],
            device_id=(dp, owners[i]), device_id_type=MESH)

    def all_blocks(c):
        blocks = pl.ds(0, NP)
        return pltpu.make_async_remote_copy(
            src_ref=stage.at[c, blocks], dst_ref=inc.at[c, blocks], send_sem=a_ss, recv_sem=a_rs.at[c],
            device_id=(dp, owners[0]), device_id_type=MESH)

    def send_blocks(c):
        rows = pl.ds(pl.multiple_of((c // NCOL) * RB, RB), RB)
        cols = pl.ds(pl.multiple_of((c % NCOL) * CW, CW), CW)
        for i in range(NP):
            stage[c, i] = grads[slot_of[i], rows, cols]
            block_copy(c, i).start()
        inc[c, NP] = grads[slot_of[NP], rows, cols]

    send_blocks(0)
    for i in range(NP):
        label_copy(i).start()

    @pl.loop(1, NC)
    def _(c):
        send_blocks(c)

    for cp in held:
        cp.start()

    pltpu.make_async_remote_copy(
        src_ref=lab_out, dst_ref=lab_in.at[pl.ds(0, NP)], send_sem=lab_ss, recv_sem=lab_rs,
        device_id=(dp, owners[0]), device_id_type=MESH).wait()
    low = jnp.full((1, CW), NOBLK, jnp.int32)
    high = jnp.full((1, CW), -1, jnp.int32)
    for i in range(NP + 1):
        lab = lab_in[i]
        low = jnp.minimum(low, jnp.where(lab < 0, NOBLK, lab))
        high = jnp.maximum(high, lab)
    two = high > low
    for i in range(NP + 1):
        lab = lab_in[i]
        weight[0, i] = jnp.where(lab == low, 1.0, 0.0)
        weight[1, i] = jnp.where((lab == high) & two, 1.0, 0.0)
    idg[dp, 0:1] = jnp.where(low < NOBLK, low, -1)[:, :128]
    idg[dp, 1:2] = jnp.where(two, high, -1)[:, :128]
    idg[NREP] = jnp.full((2, 128), step_ref[0], jnp.int32)

    def id_copy(j):
        dz, dc = dp_peers[j]
        return pltpu.make_async_remote_copy(
            src_ref=idg.at[dp], dst_ref=idg.at[dp], send_sem=id_ss, recv_sem=id_rs,
            device_id=(rep_peer(dz, dc), tb), device_id_type=MESH)

    for j in range(len(dp_peers)):
        id_copy(j).start()

    def ring_copy(c, dz):
        return pltpu.make_async_remote_copy(
            src_ref=gath.at[c, dp], dst_ref=gath.at[c, dp], send_sem=b_ss, recv_sem=b_rs.at[c, dz - 1],
            device_id=(rep_peer(dz, 0), tb), device_id_type=MESH)

    def core_copy(c, dz):
        origin = rep_peer(dz, 0)
        return pltpu.make_async_remote_copy(
            src_ref=gath.at[c, origin], dst_ref=gath.at[c, origin], send_sem=s_ss, recv_sem=s_rs,
            device_id=(rep_peer(0, 1), tb), device_id_type=MESH)

    def last_copy(j):
        dz, dc = dp_peers[j]
        return pltpu.make_async_remote_copy(
            src_ref=gath.at[NC - 1, dp], dst_ref=gath.at[NC - 1, dp], send_sem=l_ss, recv_sem=l_rs,
            device_id=(rep_peer(dz, dc), tb), device_id_type=MESH)

    def second_hop(c):
        for dz in (1, 3, 2):
            ring_copy(c, dz).wait_recv()
            core_copy(c, NSIDE - dz).start()

    @pl.loop(0, NC)
    def _(c):
        all_blocks(c).wait_recv()
        sum_low = jnp.zeros((RB, CW), jnp.float32)
        sum_high = jnp.zeros((RB, CW), jnp.float32)
        for i in range(NP + 1):
            block = inc[c, i].astype(jnp.float32)
            sum_low += weight[0, i] * block
            sum_high += weight[1, i] * block
        gath[c, dp, 0] = sum_low
        gath[c, dp, 1] = sum_high

        @pl.when(c < NC - 1)
        def _():
            for dz in (1, 3, 2):
                ring_copy(c, dz).start()
            core_copy(c, 0).start()

        @pl.when(c == NC - 1)
        def _():
            for j in LAST:
                last_copy(j).start()

        @pl.when(c >= LAG)
        def _():
            second_hop(c - LAG)

    @pl.loop(NC - LAG, NC - 1)
    def _(c):
        second_hop(c)

    others = pl.ds(0, NREP - 1)
    pltpu.make_async_remote_copy(
        src_ref=idg.at[others], dst_ref=idg.at[others], send_sem=id_ss, recv_sem=id_rs,
        device_id=(rep_peer(0, 1), tb), device_id_type=MESH).wait()
    for cp in held:
        cp.wait()

    early = pl.ds(0, NC - 1)
    ring_sent = gath.at[early, pl.ds(0, NSIDE - 1)]
    core_sent = gath.at[early, pl.ds(0, NSIDE)]
    last_sent = gath.at[NC - 1, others]
    for src, send_sem in ((ring_sent, b_ss), (stage, a_ss)):
        pltpu.make_async_remote_copy(
            src_ref=src, dst_ref=src, send_sem=send_sem, recv_sem=s_rs,
            device_id=(rep_peer(0, 1), tb), device_id_type=MESH).wait_send()
    for src, send_sem, recv_sem in ((core_sent, s_ss, s_rs), (last_sent, l_ss, l_rs)):
        pltpu.make_async_remote_copy(
            src_ref=src, dst_ref=src, send_sem=send_sem, recv_sem=recv_sem,
            device_id=(rep_peer(0, 1), tb), device_id_type=MESH).wait()


def adam_kernel(
    ids_ref, gath, values, first, second,
    out_v, out_f, out_s,
    tmp, new_v, new_f, new_s, count, names, sem,
):
    nblk = values.shape[0] // BROWS
    for b in range(nblk + 1):
        count[b] = 0
    for q in range(2 * NREP):
        named = ids_ref[q // 2, q % 2, 0]
        b = jnp.where(named < 0, nblk, named)
        n = count[b]
        names[b * 2 * NREP + n] = q
        count[b] = n + 1

    steps = ids_ref[NREP, 0, 0]
    power_one, power_two = lax.fori_loop(
        0, steps, lambda _, p: (p[0] * 0.9, p[1] * 0.99), (jnp.float32(1.0), jnp.float32(1.0)))
    one = jnp.full((1, CW), 1.0 - power_one, jnp.float32)
    two = jnp.full((1, CW), 1.0 - power_two, jnp.float32)
    rate = 0.05 / one
    scale = 1.0 / two

    def copies(b, v, f, s):
        rows = pl.ds(pl.multiple_of(b * BROWS, BROWS), BROWS)
        return [
            pltpu.make_async_copy(v.at[rows], out_v.at[rows], sem.at[0, b]),
            pltpu.make_async_copy(f.at[rows], out_f.at[rows], sem.at[1, b]),
            pltpu.make_async_copy(s.at[rows], out_s.at[rows], sem.at[2, b]),
        ]

    def update(b, grad_of):
        for c in range(NC):
            rows = pl.ds(pl.multiple_of(b * BROWS + (c // NCOL) * RB, RB), RB)
            cols = slice((c % NCOL) * CW, (c % NCOL + 1) * CW)
            g = grad_of(c)
            f = 0.9 * first[rows, cols] + (1.0 - 0.9) * g
            s = 0.99 * second[rows, cols] + (1.0 - 0.99) * g * g
            new_f[rows, cols] = f
            new_s[rows, cols] = s
            moved = values[rows, cols].astype(jnp.float32) - rate * f / (jnp.sqrt(scale * s) + 1e-08)
            new_v[rows, cols] = moved.astype(jnp.bfloat16)
        for cp in copies(b, new_v, new_f, new_s):
            cp.start()

    @pl.loop(0, nblk)
    def _(b):
        @pl.when(count[b] == 0)
        def _():
            for cp in copies(b, values, first, second):
                cp.start()

    @pl.loop(0, nblk)
    def _(b):
        n = count[b]
        base = b * 2 * NREP

        def name_of(j):
            q = names[base + j]
            return q >> 1, q & 1

        @pl.when(n == 1)
        def _():
            r, k = name_of(0)
            update(b, lambda c: gath[c, r, k])

        @pl.when(n > 1)
        def _():
            r, k = name_of(0)
            r1, k1 = name_of(1)
            for c in range(NC):
                tmp[c] = gath[c, r, k] + gath[c, r1, k1]

            def more(j, _):
                rj, kj = name_of(j)
                for c in range(NC):
                    tmp[c] += gath[c, rj, kj]
                return 0

            lax.fori_loop(2, n, more, 0)
            update(b, lambda c: tmp[c])

    @pl.loop(0, nblk)
    def _(b):
        for cp in copies(b, new_v, new_f, new_s):
            cp.wait()


def per_device(values, first_moment, second_moment, grads, block_ids, live_counts, step_count):
    own_rows, width = values.shape
    nblk = own_rows // BROWS
    dma = pltpu.SemaphoreType.DMA
    vmem = pl.BlockSpec(memory_space=pltpu.VMEM)
    smem = pl.BlockSpec(memory_space=pltpu.SMEM)
    hbm = pl.BlockSpec(memory_space=pltpu.HBM)
    like = lambda a: jax.ShapeDtypeStruct(a.shape, a.dtype)
    gath, ids, values_in, first_in, second_in = pl.pallas_call(
        exchange_kernel,
        out_shape=(
            jax.ShapeDtypeStruct((NC, NREP, 2, RB, CW), jnp.float32),
            jax.ShapeDtypeStruct((NREP + 1, 2, 128), jnp.int32),
            like(values), like(first_moment), like(second_moment),
        ),
        in_specs=[smem, smem] + [hbm] * 5,
        out_specs=(vmem,) * 5,
        scratch_shapes=[
            pltpu.SMEM(block_ids.shape, jnp.int32),
            pltpu.VMEM((SLOTS, BROWS, width), jnp.bfloat16),
            pltpu.VMEM((NC, NP, RB, CW), jnp.bfloat16),
            pltpu.VMEM((NC, NP + 1, RB, CW), jnp.bfloat16),
            pltpu.VMEM((NP, 1, CW), jnp.int32),
            pltpu.VMEM((NP + 1, 1, CW), jnp.int32),
            pltpu.VMEM((2, NP + 1, 1, CW), jnp.float32),
            dma((1,)), dma((4,)), dma(()), dma(()), dma(()), dma((NC,)),
            dma(()), dma(()), dma(()), dma((NC, NSIDE - 1)), dma(()), dma(()), dma(()), dma(()),
        ],
        compiler_params=pltpu.CompilerParams(
            collective_id=0, has_side_effects=True, vmem_limit_bytes=24 << 20),
        name="exchange",
    )(live_counts, step_count, *[pltpu.with_memory_space_constraint(a, pltpu.HBM) for a in (block_ids, grads, values, first_moment, second_moment)])
    return pl.pallas_call(
        adam_kernel,
        out_shape=(like(values), like(first_moment), like(second_moment)),
        in_specs=[smem, vmem, vmem, vmem, vmem],
        out_specs=(hbm, hbm, hbm),
        scratch_shapes=[
            pltpu.VMEM((NC, RB, CW), jnp.float32),
            pltpu.VMEM((own_rows, width), jnp.bfloat16),
            pltpu.VMEM((own_rows, width), jnp.float32),
            pltpu.VMEM((own_rows, width), jnp.float32),
            pltpu.SMEM((nblk + 1,), jnp.int32),
            pltpu.SMEM(((nblk + 1) * 2 * NREP,), jnp.int32),
            dma((3, nblk)),
        ],
        compiler_params=pltpu.CompilerParams(vmem_limit_bytes=24 << 20),
        name="adam",
    )(ids, gath, values_in, first_in, second_in)


def solution(mesh):
    in_specs = (
        P("table", None),
        P("table", None),
        P("table", None),
        P(("dp", "table"), None, None),
        P(("dp", "table"), None),
        P(("dp", "table")),
        P(),
    )
    out_specs = (P("table", None), P("table", None), P("table", None))
    return jax.shard_map(
        per_device, mesh=mesh, in_specs=in_specs, out_specs=out_specs, check_vma=False
    )
```

```python
import jax
import jax.numpy as jnp
from jax import lax
from jax.experimental import pallas as pl
from jax.experimental.pallas import tpu as pltpu
from jax.sharding import PartitionSpec as P

MESH = pl.DeviceIdType.MESH
BROWS = 64
SLOTS = 8
NSIDE = 4
RB = 16
CW = 256
NROW = BROWS // RB
NCOL = 1024 // CW
NC = NROW * NCOL
DIRECT = 1
MAIN = NC - DIRECT
PLANE = [(2, 2), (1, 2), (3, 2), (2, 1), (2, 3), (1, 1), (3, 3), (1, 3), (3, 1), (0, 2), (2, 0), (0, 1), (0, 3), (1, 0), (3, 0)]
NP = len(PLANE)
NREP = 8
LAST = (4, 3, 2, 5, 1, 6, 0)
LAG = 4
NOBLK = 1 << 20


def exchange_kernel(
    cnt_ref, step_ref, ids_hbm, grads_hbm, values_hbm, first_hbm, second_hbm,
    gath, idg, values, first, second,
    ids_ref, grads, stage, inc, lab_out, lab_in, weight,
    sm_sem, ld_sem, lab_ss, lab_rs, a_ss, a_rs, id_ss, id_rs, b_ss, b_rs, s_ss, s_rs, l_ss, l_rs,
):
    dp = lax.axis_index("dp")
    tb = lax.axis_index("table")
    z, core = dp // 2, dp % 2
    x, y = tb // NSIDE, tb % NSIDE

    def plane_peer(i):
        dx, dy = PLANE[i]
        return ((x + dx) % NSIDE) * NSIDE + (y + dy) % NSIDE

    def rep_peer(dz, dc):
        return ((z + dz) % NSIDE) * 2 + (core + dc) % 2

    owners = [plane_peer(i) for i in range(NP)] + [tb]
    dp_peers = [(dz, dc) for dz in range(NSIDE) for dc in range(2) if (dz, dc) != (0, 0)]

    small = [
        pltpu.make_async_copy(ids_hbm, ids_ref, sm_sem.at[0]),
    ]
    load = pltpu.make_async_copy(grads_hbm, grads, ld_sem.at[0])
    held = [
        pltpu.make_async_copy(values_hbm, values, ld_sem.at[1]),
        pltpu.make_async_copy(first_hbm, first, ld_sem.at[2]),
        pltpu.make_async_copy(second_hbm, second, ld_sem.at[3]),
    ]
    barrier = pltpu.get_barrier_semaphore()
    for i in range(NP):
        pl.semaphore_signal(barrier, inc=1, device_id=(dp, owners[i]), device_id_type=MESH)
    for dz, dc in dp_peers:
        pl.semaphore_signal(barrier, inc=1, device_id=(rep_peer(dz, dc), tb), device_id_type=MESH)

    for cp in small:
        cp.start()
    load.start()
    for cp in small:
        cp.wait()
    count = cnt_ref[0]
    named = [jnp.where(s < count, ids_ref[0, s], NOBLK) for s in range(SLOTS)]
    slot_of = []
    for i in range(NP + 1):
        slot = jnp.int32(0)
        label = jnp.int32(-1)
        for s in range(SLOTS):
            here = (named[s] >> 4) == owners[i]
            slot = jnp.where(here, s, slot)
            label = jnp.where(here, named[s] & 15, label)
        slot_of.append(slot)
        row = jnp.full((1, CW), label, jnp.int32)
        if i < NP:
            lab_out[i] = row
        else:
            lab_in[i] = row

    load.wait()
    pl.semaphore_wait(barrier, NP + len(dp_peers))

    def label_copy(i):
        return pltpu.make_async_remote_copy(
            src_ref=lab_out.at[i], dst_ref=lab_in.at[i], send_sem=lab_ss, recv_sem=lab_rs,
            device_id=(dp, owners[i]), device_id_type=MESH)

    def block_copy(c, i):
        return pltpu.make_async_remote_copy(
            src_ref=stage.at[c, i], dst_ref=inc.at[c, i], send_sem=a_ss, recv_sem=a_rs.at[c],
            device_id=(dp, owners[i]), device_id_type=MESH)

    def all_blocks(c):
        blocks = pl.ds(0, NP)
        return pltpu.make_async_remote_copy(
            src_ref=stage.at[c, blocks], dst_ref=inc.at[c, blocks], send_sem=a_ss, recv_sem=a_rs.at[c],
            device_id=(dp, owners[0]), device_id_type=MESH)

    def send_blocks(c):
        rows = pl.ds(pl.multiple_of((c // NCOL) * RB, RB), RB)
        cols = pl.ds(pl.multiple_of((c % NCOL) * CW, CW), CW)
        for i in range(NP):
            stage[c, i] = grads[slot_of[i], rows, cols]
            block_copy(c, i).start()
        inc[c, NP] = grads[slot_of[NP], rows, cols]

    for i in range(NP):
        label_copy(i).start()
    send_blocks(0)

    @pl.loop(1, NC)
    def _(c):
        send_blocks(c)

    for cp in held:
        cp.start()

    pltpu.make_async_remote_copy(
        src_ref=lab_out, dst_ref=lab_in.at[pl.ds(0, NP)], send_sem=lab_ss, recv_sem=lab_rs,
        device_id=(dp, owners[0]), device_id_type=MESH).wait()
    low = jnp.full((1, CW), NOBLK, jnp.int32)
    high = jnp.full((1, CW), -1, jnp.int32)
    for i in range(NP + 1):
        lab = lab_in[i]
        low = jnp.minimum(low, jnp.where(lab < 0, NOBLK, lab))
        high = jnp.maximum(high, lab)
    two = high > low
    for i in range(NP + 1):
        lab = lab_in[i]
        weight[0, i] = jnp.where(lab == low, 1.0, 0.0)
        weight[1, i] = jnp.where((lab == high) & two, 1.0, 0.0)
    idg[dp, 0:1] = jnp.where(low < NOBLK, low, -1)[:, :128]
    idg[dp, 1:2] = jnp.where(two, high, -1)[:, :128]
    idg[NREP] = jnp.full((2, 128), step_ref[0], jnp.int32)

    def id_copy(j):
        dz, dc = dp_peers[j]
        return pltpu.make_async_remote_copy(
            src_ref=idg.at[dp], dst_ref=idg.at[dp], send_sem=id_ss, recv_sem=id_rs,
            device_id=(rep_peer(dz, dc), tb), device_id_type=MESH)

    for j in range(len(dp_peers)):
        id_copy(j).start()

    def ring_copy(c, dz):
        return pltpu.make_async_remote_copy(
            src_ref=gath.at[c, dp], dst_ref=gath.at[c, dp], send_sem=b_ss, recv_sem=b_rs.at[c, dz - 1],
            device_id=(rep_peer(dz, 0), tb), device_id_type=MESH)

    def core_copy(c, dz):
        origin = rep_peer(dz, 0)
        return pltpu.make_async_remote_copy(
            src_ref=gath.at[c, origin], dst_ref=gath.at[c, origin], send_sem=s_ss, recv_sem=s_rs,
            device_id=(rep_peer(0, 1), tb), device_id_type=MESH)

    def last_copy(c, j):
        dz, dc = dp_peers[j]
        return pltpu.make_async_remote_copy(
            src_ref=gath.at[c, dp], dst_ref=gath.at[c, dp], send_sem=l_ss, recv_sem=l_rs,
            device_id=(rep_peer(dz, dc), tb), device_id_type=MESH)

    def second_hop(c):
        for dz in (1, 3, 2):
            ring_copy(c, dz).wait_recv()
            core_copy(c, NSIDE - dz).start()

    @pl.loop(0, NC)
    def _(c):
        all_blocks(c).wait_recv()
        sum_low = jnp.zeros((RB, CW), jnp.float32)
        sum_high = jnp.zeros((RB, CW), jnp.float32)
        for i in range(NP + 1):
            block = inc[c, i].astype(jnp.float32)
            sum_low += weight[0, i] * block
            sum_high += weight[1, i] * block
        gath[c, dp, 0] = sum_low
        gath[c, dp, 1] = sum_high

        @pl.when(c < MAIN)
        def _():
            for dz in (1, 3, 2):
                ring_copy(c, dz).start()
            core_copy(c, 0).start()

        @pl.when(c >= MAIN)
        def _():
            for j in LAST:
                last_copy(c, j).start()

        @pl.when(c >= LAG)
        def _():
            second_hop(c - LAG)

    @pl.loop(NC - LAG, MAIN)
    def _(c):
        second_hop(c)

    others = pl.ds(0, NREP - 1)
    pltpu.make_async_remote_copy(
        src_ref=idg.at[others], dst_ref=idg.at[others], send_sem=id_ss, recv_sem=id_rs,
        device_id=(rep_peer(0, 1), tb), device_id_type=MESH).wait()
    for cp in held:
        cp.wait()

    early = pl.ds(0, MAIN)
    ring_sent = gath.at[early, pl.ds(0, NSIDE - 1)]
    core_sent = gath.at[early, pl.ds(0, NSIDE)]
    last_sent = gath.at[pl.ds(MAIN, DIRECT), others]
    for src, send_sem in ((ring_sent, b_ss), (stage, a_ss)):
        pltpu.make_async_remote_copy(
            src_ref=src, dst_ref=src, send_sem=send_sem, recv_sem=s_rs,
            device_id=(rep_peer(0, 1), tb), device_id_type=MESH).wait_send()
    for src, send_sem, recv_sem in ((core_sent, s_ss, s_rs), (last_sent, l_ss, l_rs)):
        pltpu.make_async_remote_copy(
            src_ref=src, dst_ref=src, send_sem=send_sem, recv_sem=recv_sem,
            device_id=(rep_peer(0, 1), tb), device_id_type=MESH).wait()


def adam_kernel(
    ids_ref, gath, values, first, second,
    out_v, out_f, out_s,
    tmp, new_v, new_f, new_s, count, names, sem,
):
    nblk = values.shape[0] // BROWS
    for b in range(nblk + 1):
        count[b] = 0
    for q in range(2 * NREP):
        named = ids_ref[q // 2, q % 2, 0]
        b = jnp.where(named < 0, nblk, named)
        n = count[b]
        names[b * 2 * NREP + n] = q
        count[b] = n + 1

    steps = ids_ref[NREP, 0, 0]
    power_one, power_two = lax.fori_loop(
        0, steps, lambda _, p: (p[0] * 0.9, p[1] * 0.99), (jnp.float32(1.0), jnp.float32(1.0)))
    one = jnp.full((1, CW), 1.0 - power_one, jnp.float32)
    two = jnp.full((1, CW), 1.0 - power_two, jnp.float32)
    rate = 0.05 / one
    scale = 1.0 / two

    def copies(b, v, f, s):
        rows = pl.ds(pl.multiple_of(b * BROWS, BROWS), BROWS)
        return [
            pltpu.make_async_copy(v.at[rows], out_v.at[rows], sem.at[0, b]),
            pltpu.make_async_copy(f.at[rows], out_f.at[rows], sem.at[1, b]),
            pltpu.make_async_copy(s.at[rows], out_s.at[rows], sem.at[2, b]),
        ]

    def update(b, grad_of):
        for c in range(NC):
            rows = pl.ds(pl.multiple_of(b * BROWS + (c // NCOL) * RB, RB), RB)
            cols = slice((c % NCOL) * CW, (c % NCOL + 1) * CW)
            g = grad_of(c)
            f = 0.9 * first[rows, cols] + (1.0 - 0.9) * g
            s = 0.99 * second[rows, cols] + (1.0 - 0.99) * g * g
            new_f[rows, cols] = f
            new_s[rows, cols] = s
            moved = values[rows, cols].astype(jnp.float32) - rate * f / (jnp.sqrt(scale * s) + 1e-08)
            new_v[rows, cols] = moved.astype(jnp.bfloat16)
        for cp in copies(b, new_v, new_f, new_s):
            cp.start()

    @pl.loop(0, nblk)
    def _(b):
        @pl.when(count[b] == 0)
        def _():
            for cp in copies(b, values, first, second):
                cp.start()

    @pl.loop(0, nblk)
    def _(b):
        n = count[b]
        base = b * 2 * NREP

        def name_of(j):
            q = names[base + j]
            return q >> 1, q & 1

        @pl.when(n == 1)
        def _():
            r, k = name_of(0)
            update(b, lambda c: gath[c, r, k])

        @pl.when(n > 1)
        def _():
            r, k = name_of(0)
            r1, k1 = name_of(1)
            for c in range(NC):
                tmp[c] = gath[c, r, k] + gath[c, r1, k1]

            def more(j, _):
                rj, kj = name_of(j)
                for c in range(NC):
                    tmp[c] += gath[c, rj, kj]
                return 0

            lax.fori_loop(2, n, more, 0)
            update(b, lambda c: tmp[c])

    @pl.loop(0, nblk)
    def _(b):
        for cp in copies(b, new_v, new_f, new_s):
            cp.wait()


def per_device(values, first_moment, second_moment, grads, block_ids, live_counts, step_count):
    own_rows, width = values.shape
    nblk = own_rows // BROWS
    dma = pltpu.SemaphoreType.DMA
    vmem = pl.BlockSpec(memory_space=pltpu.VMEM)
    smem = pl.BlockSpec(memory_space=pltpu.SMEM)
    hbm = pl.BlockSpec(memory_space=pltpu.HBM)
    like = lambda a: jax.ShapeDtypeStruct(a.shape, a.dtype)
    gath, ids, values_in, first_in, second_in = pl.pallas_call(
        exchange_kernel,
        out_shape=(
            jax.ShapeDtypeStruct((NC, NREP, 2, RB, CW), jnp.float32),
            jax.ShapeDtypeStruct((NREP + 1, 2, 128), jnp.int32),
            like(values), like(first_moment), like(second_moment),
        ),
        in_specs=[smem, smem] + [hbm] * 5,
        out_specs=(vmem,) * 5,
        scratch_shapes=[
            pltpu.SMEM(block_ids.shape, jnp.int32),
            pltpu.VMEM((SLOTS, BROWS, width), jnp.bfloat16),
            pltpu.VMEM((NC, NP, RB, CW), jnp.bfloat16),
            pltpu.VMEM((NC, NP + 1, RB, CW), jnp.bfloat16),
            pltpu.VMEM((NP, 1, CW), jnp.int32),
            pltpu.VMEM((NP + 1, 1, CW), jnp.int32),
            pltpu.VMEM((2, NP + 1, 1, CW), jnp.float32),
            dma((1,)), dma((4,)), dma(()), dma(()), dma(()), dma((NC,)),
            dma(()), dma(()), dma(()), dma((NC, NSIDE - 1)), dma(()), dma(()), dma(()), dma(()),
        ],
        compiler_params=pltpu.CompilerParams(
            collective_id=0, has_side_effects=True, vmem_limit_bytes=24 << 20),
        name="exchange",
    )(live_counts, step_count, *[pltpu.with_memory_space_constraint(a, pltpu.HBM) for a in (block_ids, grads, values, first_moment, second_moment)])
    return pl.pallas_call(
        adam_kernel,
        out_shape=(like(values), like(first_moment), like(second_moment)),
        in_specs=[smem, vmem, vmem, vmem, vmem],
        out_specs=(hbm, hbm, hbm),
        scratch_shapes=[
            pltpu.VMEM((NC, RB, CW), jnp.float32),
            pltpu.VMEM((own_rows, width), jnp.bfloat16),
            pltpu.VMEM((own_rows, width), jnp.float32),
            pltpu.VMEM((own_rows, width), jnp.float32),
            pltpu.SMEM((nblk + 1,), jnp.int32),
            pltpu.SMEM(((nblk + 1) * 2 * NREP,), jnp.int32),
            dma((3, nblk)),
        ],
        compiler_params=pltpu.CompilerParams(vmem_limit_bytes=24 << 20),
        name="adam",
    )(ids, gath, values_in, first_in, second_in)


def solution(mesh):
    in_specs = (
        P("table", None),
        P("table", None),
        P("table", None),
        P(("dp", "table"), None, None),
        P(("dp", "table"), None),
        P(("dp", "table")),
        P(),
    )
    out_specs = (P("table", None), P("table", None), P("table", None))
    return jax.shard_map(
        per_device, mesh=mesh, in_specs=in_specs, out_specs=out_specs, check_vma=False
    )
```

```python
import jax
import jax.numpy as jnp
from jax import lax
from jax.experimental import pallas as pl
from jax.experimental.pallas import tpu as pltpu
from jax.sharding import PartitionSpec as P

MESH = pl.DeviceIdType.MESH
BROWS = 64
SLOTS = 8
NSIDE = 4
RB = 16
CW = 256
NROW = BROWS // RB
NCOL = 1024 // CW
NC = NROW * NCOL
DIRECT = 1
MAIN = NC - DIRECT
PLANE = [(2, 2), (1, 2), (3, 2), (2, 1), (2, 3), (1, 1), (3, 3), (1, 3), (3, 1), (0, 2), (2, 0), (0, 1), (0, 3), (1, 0), (3, 0)]
NP = len(PLANE)
NREP = 8
LAST = (4, 3, 2, 5, 1, 6, 0)
LAG = 4
NOBLK = 1 << 20


def exchange_kernel(
    cnt_ref, step_ref, ids_hbm, grads_hbm, values_hbm, first_hbm, second_hbm,
    gath, idg, values, first, second,
    ids_ref, grads, stage, inc, lab_out, lab_in, weight,
    sm_sem, ld_sem, lab_ss, lab_rs, a_ss, a_rs, id_ss, id_rs, b_ss, b_rs, s_ss, s_rs, l_ss, l_rs,
):
    dp = lax.axis_index("dp")
    tb = lax.axis_index("table")
    z, core = dp // 2, dp % 2
    x, y = tb // NSIDE, tb % NSIDE

    def plane_peer(i):
        dx, dy = PLANE[i]
        return ((x + dx) % NSIDE) * NSIDE + (y + dy) % NSIDE

    def rep_peer(dz, dc):
        return ((z + dz) % NSIDE) * 2 + (core + dc) % 2

    owners = [plane_peer(i) for i in range(NP)] + [tb]
    dp_peers = [(dz, dc) for dz in range(NSIDE) for dc in range(2) if (dz, dc) != (0, 0)]

    small = [
        pltpu.make_async_copy(ids_hbm, ids_ref, sm_sem.at[0]),
    ]
    load = pltpu.make_async_copy(grads_hbm, grads, ld_sem.at[0])
    held = [
        pltpu.make_async_copy(values_hbm, values, ld_sem.at[1]),
        pltpu.make_async_copy(first_hbm, first, ld_sem.at[2]),
        pltpu.make_async_copy(second_hbm, second, ld_sem.at[3]),
    ]
    barrier = pltpu.get_barrier_semaphore()
    for i in range(NP):
        pl.semaphore_signal(barrier, inc=1, device_id=(dp, owners[i]), device_id_type=MESH)
    for dz, dc in dp_peers:
        pl.semaphore_signal(barrier, inc=1, device_id=(rep_peer(dz, dc), tb), device_id_type=MESH)

    for cp in small:
        cp.start()
    load.start()
    for cp in small:
        cp.wait()
    count = cnt_ref[0]
    named = [jnp.where(s < count, ids_ref[0, s], NOBLK) for s in range(SLOTS)]
    slot_of = []
    for i in range(NP + 1):
        slot = jnp.int32(0)
        label = jnp.int32(-1)
        for s in range(SLOTS):
            here = (named[s] >> 4) == owners[i]
            slot = jnp.where(here, s, slot)
            label = jnp.where(here, named[s] & 15, label)
        slot_of.append(slot)
        row = jnp.full((1, CW), label, jnp.int32)
        if i < NP:
            lab_out[i] = row
        else:
            lab_in[i] = row

    load.wait()
    pl.semaphore_wait(barrier, NP + len(dp_peers))

    def label_copy(i):
        return pltpu.make_async_remote_copy(
            src_ref=lab_out.at[i], dst_ref=lab_in.at[i], send_sem=lab_ss, recv_sem=lab_rs,
            device_id=(dp, owners[i]), device_id_type=MESH)

    def block_copy(c, i):
        return pltpu.make_async_remote_copy(
            src_ref=stage.at[c, i], dst_ref=inc.at[c, i], send_sem=a_ss, recv_sem=a_rs.at[c],
            device_id=(dp, owners[i]), device_id_type=MESH)

    def all_blocks(c):
        blocks = pl.ds(0, NP)
        return pltpu.make_async_remote_copy(
            src_ref=stage.at[c, blocks], dst_ref=inc.at[c, blocks], send_sem=a_ss, recv_sem=a_rs.at[c],
            device_id=(dp, owners[0]), device_id_type=MESH)

    def send_blocks(c):
        rows = pl.ds(pl.multiple_of((c // NCOL) * RB, RB), RB)
        cols = pl.ds(pl.multiple_of((c % NCOL) * CW, CW), CW)
        for i in range(NP):
            stage[c, i] = grads[slot_of[i], rows, cols]
            block_copy(c, i).start()
        inc[c, NP] = grads[slot_of[NP], rows, cols]

    for i in range(NP):
        label_copy(i).start()
    send_blocks(0)

    @pl.loop(1, NC)
    def _(c):
        send_blocks(c)

    for cp in held:
        cp.start()

    pltpu.make_async_remote_copy(
        src_ref=lab_out, dst_ref=lab_in.at[pl.ds(0, NP)], send_sem=lab_ss, recv_sem=lab_rs,
        device_id=(dp, owners[0]), device_id_type=MESH).wait()
    low = jnp.full((1, CW), NOBLK, jnp.int32)
    high = jnp.full((1, CW), -1, jnp.int32)
    for i in range(NP + 1):
        lab = lab_in[i]
        low = jnp.minimum(low, jnp.where(lab < 0, NOBLK, lab))
        high = jnp.maximum(high, lab)
    two = high > low
    for i in range(NP + 1):
        lab = lab_in[i]
        weight[0, i] = jnp.where(lab == low, 1.0, 0.0)
        weight[1, i] = jnp.where((lab == high) & two, 1.0, 0.0)
    idg[dp, 0:1] = jnp.where(low < NOBLK, low, -1)[:, :128]
    idg[dp, 1:2] = jnp.where(two, high, -1)[:, :128]
    idg[NREP] = jnp.full((2, 128), step_ref[0], jnp.int32)

    def id_copy(j):
        dz, dc = dp_peers[j]
        return pltpu.make_async_remote_copy(
            src_ref=idg.at[dp], dst_ref=idg.at[dp], send_sem=id_ss, recv_sem=id_rs,
            device_id=(rep_peer(dz, dc), tb), device_id_type=MESH)

    for j in range(len(dp_peers)):
        id_copy(j).start()

    def ring_copy(c, dz):
        return pltpu.make_async_remote_copy(
            src_ref=gath.at[c, dp], dst_ref=gath.at[c, dp], send_sem=b_ss, recv_sem=b_rs.at[c, dz - 1],
            device_id=(rep_peer(dz, 0), tb), device_id_type=MESH)

    def core_copy(c, dz):
        origin = rep_peer(dz, 0)
        return pltpu.make_async_remote_copy(
            src_ref=gath.at[c, origin], dst_ref=gath.at[c, origin], send_sem=s_ss, recv_sem=s_rs,
            device_id=(rep_peer(0, 1), tb), device_id_type=MESH)

    def last_copy(c, j):
        dz, dc = dp_peers[j]
        return pltpu.make_async_remote_copy(
            src_ref=gath.at[c, dp], dst_ref=gath.at[c, dp], send_sem=l_ss, recv_sem=l_rs,
            device_id=(rep_peer(dz, dc), tb), device_id_type=MESH)

    def second_hop(c):
        for dz in (1, 3, 2):
            ring_copy(c, dz).wait_recv()
            core_copy(c, NSIDE - dz).start()

    @pl.loop(0, NC)
    def _(c):
        all_blocks(c).wait_recv()
        sum_low = jnp.zeros((RB, CW), jnp.float32)
        sum_high = jnp.zeros((RB, CW), jnp.float32)
        for i in range(NP + 1):
            block = inc[c, i].astype(jnp.float32)
            sum_low += weight[0, i] * block
            sum_high += weight[1, i] * block
        gath[c, dp, 0] = sum_low
        gath[c, dp, 1] = sum_high

        @pl.when(c < MAIN)
        def _():
            for dz in (1, 3, 2):
                ring_copy(c, dz).start()
            core_copy(c, 0).start()

        @pl.when(c >= MAIN)
        def _():
            for j in LAST:
                last_copy(c, j).start()

        @pl.when(c >= LAG)
        def _():
            second_hop(c - LAG)


    others = pl.ds(0, NREP - 1)
    pltpu.make_async_remote_copy(
        src_ref=idg.at[others], dst_ref=idg.at[others], send_sem=id_ss, recv_sem=id_rs,
        device_id=(rep_peer(0, 1), tb), device_id_type=MESH).wait()
    for cp in held:
        cp.wait()

    @pl.loop(NC - LAG, MAIN)
    def _(c):
        second_hop(c)

    early = pl.ds(0, MAIN)
    ring_sent = gath.at[early, pl.ds(0, NSIDE - 1)]
    core_sent = gath.at[early, pl.ds(0, NSIDE)]
    last_sent = gath.at[pl.ds(MAIN, DIRECT), others]
    for src, send_sem in ((ring_sent, b_ss), (stage, a_ss)):
        pltpu.make_async_remote_copy(
            src_ref=src, dst_ref=src, send_sem=send_sem, recv_sem=s_rs,
            device_id=(rep_peer(0, 1), tb), device_id_type=MESH).wait_send()
    for src, send_sem, recv_sem in ((core_sent, s_ss, s_rs), (last_sent, l_ss, l_rs)):
        pltpu.make_async_remote_copy(
            src_ref=src, dst_ref=src, send_sem=send_sem, recv_sem=recv_sem,
            device_id=(rep_peer(0, 1), tb), device_id_type=MESH).wait()


def adam_kernel(
    ids_ref, gath, values, first, second,
    out_v, out_f, out_s,
    tmp, new_v, new_f, new_s, count, names, sem,
):
    nblk = values.shape[0] // BROWS
    for b in range(nblk + 1):
        count[b] = 0
    for q in range(2 * NREP):
        named = ids_ref[q // 2, q % 2, 0]
        b = jnp.where(named < 0, nblk, named)
        n = count[b]
        names[b * 2 * NREP + n] = q
        count[b] = n + 1

    steps = ids_ref[NREP, 0, 0]
    power_one, power_two = lax.fori_loop(
        0, steps, lambda _, p: (p[0] * 0.9, p[1] * 0.99), (jnp.float32(1.0), jnp.float32(1.0)))
    one = jnp.full((1, CW), 1.0 - power_one, jnp.float32)
    two = jnp.full((1, CW), 1.0 - power_two, jnp.float32)
    rate = 0.05 / one
    scale = 1.0 / two

    def copies(b, v, f, s):
        rows = pl.ds(pl.multiple_of(b * BROWS, BROWS), BROWS)
        return [
            pltpu.make_async_copy(v.at[rows], out_v.at[rows], sem.at[0, b]),
            pltpu.make_async_copy(f.at[rows], out_f.at[rows], sem.at[1, b]),
            pltpu.make_async_copy(s.at[rows], out_s.at[rows], sem.at[2, b]),
        ]

    def update(b, grad_of):
        for c in range(NC):
            rows = pl.ds(pl.multiple_of(b * BROWS + (c // NCOL) * RB, RB), RB)
            cols = slice((c % NCOL) * CW, (c % NCOL + 1) * CW)
            g = grad_of(c)
            f = 0.9 * first[rows, cols] + (1.0 - 0.9) * g
            s = 0.99 * second[rows, cols] + (1.0 - 0.99) * g * g
            new_f[rows, cols] = f
            new_s[rows, cols] = s
            moved = values[rows, cols].astype(jnp.float32) - rate * f / (jnp.sqrt(scale * s) + 1e-08)
            new_v[rows, cols] = moved.astype(jnp.bfloat16)
        for cp in copies(b, new_v, new_f, new_s):
            cp.start()

    @pl.loop(0, nblk)
    def _(b):
        @pl.when(count[b] == 0)
        def _():
            for cp in copies(b, values, first, second):
                cp.start()

    @pl.loop(0, nblk)
    def _(b):
        n = count[b]
        base = b * 2 * NREP

        def name_of(j):
            q = names[base + j]
            return q >> 1, q & 1

        @pl.when(n == 1)
        def _():
            r, k = name_of(0)
            update(b, lambda c: gath[c, r, k])

        @pl.when(n > 1)
        def _():
            r, k = name_of(0)
            r1, k1 = name_of(1)
            for c in range(NC):
                tmp[c] = gath[c, r, k] + gath[c, r1, k1]

            def more(j, _):
                rj, kj = name_of(j)
                for c in range(NC):
                    tmp[c] += gath[c, rj, kj]
                return 0

            lax.fori_loop(2, n, more, 0)
            update(b, lambda c: tmp[c])

    @pl.loop(0, nblk)
    def _(b):
        for cp in copies(b, new_v, new_f, new_s):
            cp.wait()


def per_device(values, first_moment, second_moment, grads, block_ids, live_counts, step_count):
    own_rows, width = values.shape
    nblk = own_rows // BROWS
    dma = pltpu.SemaphoreType.DMA
    vmem = pl.BlockSpec(memory_space=pltpu.VMEM)
    smem = pl.BlockSpec(memory_space=pltpu.SMEM)
    hbm = pl.BlockSpec(memory_space=pltpu.HBM)
    like = lambda a: jax.ShapeDtypeStruct(a.shape, a.dtype)
    gath, ids, values_in, first_in, second_in = pl.pallas_call(
        exchange_kernel,
        out_shape=(
            jax.ShapeDtypeStruct((NC, NREP, 2, RB, CW), jnp.float32),
            jax.ShapeDtypeStruct((NREP + 1, 2, 128), jnp.int32),
            like(values), like(first_moment), like(second_moment),
        ),
        in_specs=[smem, smem] + [hbm] * 5,
        out_specs=(vmem,) * 5,
        scratch_shapes=[
            pltpu.SMEM(block_ids.shape, jnp.int32),
            pltpu.VMEM((SLOTS, BROWS, width), jnp.bfloat16),
            pltpu.VMEM((NC, NP, RB, CW), jnp.bfloat16),
            pltpu.VMEM((NC, NP + 1, RB, CW), jnp.bfloat16),
            pltpu.VMEM((NP, 1, CW), jnp.int32),
            pltpu.VMEM((NP + 1, 1, CW), jnp.int32),
            pltpu.VMEM((2, NP + 1, 1, CW), jnp.float32),
            dma((1,)), dma((4,)), dma(()), dma(()), dma(()), dma((NC,)),
            dma(()), dma(()), dma(()), dma((NC, NSIDE - 1)), dma(()), dma(()), dma(()), dma(()),
        ],
        compiler_params=pltpu.CompilerParams(
            collective_id=0, has_side_effects=True, vmem_limit_bytes=24 << 20),
        name="exchange",
    )(live_counts, step_count, *[pltpu.with_memory_space_constraint(a, pltpu.HBM) for a in (block_ids, grads, values, first_moment, second_moment)])
    return pl.pallas_call(
        adam_kernel,
        out_shape=(like(values), like(first_moment), like(second_moment)),
        in_specs=[smem, vmem, vmem, vmem, vmem],
        out_specs=(hbm, hbm, hbm),
        scratch_shapes=[
            pltpu.VMEM((NC, RB, CW), jnp.float32),
            pltpu.VMEM((own_rows, width), jnp.bfloat16),
            pltpu.VMEM((own_rows, width), jnp.float32),
            pltpu.VMEM((own_rows, width), jnp.float32),
            pltpu.SMEM((nblk + 1,), jnp.int32),
            pltpu.SMEM(((nblk + 1) * 2 * NREP,), jnp.int32),
            dma((3, nblk)),
        ],
        compiler_params=pltpu.CompilerParams(vmem_limit_bytes=24 << 20),
        name="adam",
    )(ids, gath, values_in, first_in, second_in)


def solution(mesh):
    in_specs = (
        P("table", None),
        P("table", None),
        P("table", None),
        P(("dp", "table"), None, None),
        P(("dp", "table"), None),
        P(("dp", "table")),
        P(),
    )
    out_specs = (P("table", None), P("table", None), P("table", None))
    return jax.shard_map(
        per_device, mesh=mesh, in_specs=in_specs, out_specs=out_specs, check_vma=False
    )
```
